1024 devices in a mesh: grp: 16 (over z, core), loc: 8 (over y), tp: 8 (over x).
Axes of the slice: x: 8, y: 8, z: 8, core: 2. Of those that a mesh axis runs over, the one named last changes fastest.
Arguments:
- tokens: bfloat16 [32768, 2048], P(('grp', 'tp')), may hold values from -6 to 6
- expert_ids: int32 [32768, 8], P(('grp', 'tp')), may hold values from 0 to 127, as said below
- router_weights: bfloat16 [32768, 8], P(('grp', 'tp')), may hold values from 0.19921875 to 1
- w_gate: bfloat16 [128, 2048, 768], P(('grp', 'loc')), may hold values from -0.125 to 0.125
- w_up: bfloat16 [128, 2048, 768], P(('grp', 'loc')), may hold values from -0.125 to 0.125
- w_down: bfloat16 [128, 768, 2048], P(('grp', 'loc'), None, 'tp'), may hold values from -0.21875 to 0.21875
Outputs:
- mixed: bfloat16 [32768, 2048], P(('grp', 'tp'), 'loc')
The draws below stay inside these ranges and needn't reach their ends.
Inputs may be any that keep to these rules, and one draw needn't show every extreme that they name: `expert_ids`: each row names 8 different experts, two from each of 4 different groups, group g holding experts g * 8 to g * 8 + 7. Within each aligned block of 256 rows, no expert is named by more than 24 rows, and in every block some expert is named by exactly 24 rows.
All inputs are finite; a program needn't handle non-finite values.
Results may differ from the reference program's by a relative error of at most 0.0057.
Values may be sent and summed in bfloat16 or wider, within the bound.
A program may use at most 64 MiB of HBM per device.

```python
import math
import jax
import jax.numpy as jnp
from jax import lax

D = 2048
FF = 768
TOPK = 8
TOPG = 4
TOK_DEV = 256
TOKENS = 32768
GROUPS = 16
GROUP_SIZE = 8
EXPERTS = 128
CAP = 24


def block_routes(key):
    quantum = TOK_DEV // GROUPS
    top_lift = quantum * min(2, GROUPS - 4)
    pair_count = GROUPS // 2
    key_lift, key_label, key_extra, key_shuffle = jax.random.split(key, 4)
    lifted = jax.random.randint(key_lift, (pair_count,), 0, top_lift + 1).astype(jnp.int32)
    lifted = lifted.at[0].set(top_lift)
    group_counts = jnp.concatenate([4 * quantum + lifted, (4 * quantum - lifted)[::-1]]).astype(jnp.int32)
    group_ends = jnp.cumsum(group_counts).astype(jnp.int32)
    group_starts = group_ends - group_counts
    position = jnp.arange(TOPG * TOK_DEV, dtype=jnp.int32)
    run_index = jnp.sum((position[:, None] >= group_ends[None, :]).astype(jnp.int32), axis=1).astype(jnp.int32)
    within_run = position - group_starts[run_index]
    run_size = group_counts[run_index]
    base_load = 2 * group_counts // GROUP_SIZE
    extra_load = 2 * group_counts % GROUP_SIZE
    extra_rank = jax.vmap(lambda sub_key: jax.random.permutation(sub_key, GROUP_SIZE))(jax.random.split(key_extra, GROUPS)).astype(jnp.int32)
    expert_loads = base_load[:, None] + (extra_rank < extra_load[:, None]).astype(jnp.int32)
    run_ends = jnp.cumsum(expert_loads, axis=1).astype(jnp.int32)
    chosen_ends = run_ends[run_index]
    first_local = jnp.sum((within_run[:, None] >= chosen_ends).astype(jnp.int32), axis=1).astype(jnp.int32)
    second_local = jnp.sum(((within_run + run_size)[:, None] >= chosen_ends).astype(jnp.int32), axis=1).astype(jnp.int32)
    group_label = jax.random.permutation(key_label, GROUPS).astype(jnp.int32)
    group_id = group_label[run_index]
    pair_ids = jnp.stack([group_id * GROUP_SIZE + first_local, group_id * GROUP_SIZE + second_local], axis=-1)
    pair_ids = pair_ids.reshape(TOPG, TOK_DEV, 2).transpose(1, 0, 2).reshape(TOK_DEV, TOPK)
    shuffle = jax.random.permutation(key_shuffle, TOK_DEV)
    return pair_ids[shuffle].astype(jnp.int32)


def draw_expert_ids(key, part):
    block_count = TOKENS // TOK_DEV
    block_keys = jax.random.split(key, block_count)
    routed = jax.vmap(block_routes)(block_keys)
    return routed.reshape(TOKENS, TOPK).astype(jnp.int32)


def shard_levels(own_key, extent, shards, low, top_value):
    factor_of = 1.0
    for dim, shards_of in shards:
        heights = jax.random.uniform(jax.random.fold_in(jax.random.fold_in(own_key, 6), dim), (shards_of,), jnp.float32, low / len(shards), top_value / len(shards))
        factor_of = factor_of * jnp.repeat(jnp.exp(heights), extent[dim] // shards_of).reshape((-1,) + (1,) * (len(extent) - 1 - dim))
    return factor_of


def normal_values(own_key, shape, deviation, limit, cuts=(), kind=jnp.bfloat16):
    array = jax.random.normal(own_key, shape, jnp.float32) * deviation
    if len(cuts) > 0:
        array = shard_levels(own_key, shape, cuts, -0.22, 0.18) * array
    return jnp.clip(array, min=-limit, max=limit).astype(kind)


def setup_inputs(seed: int = 0) -> dict:
    seeds = jax.random.split(jax.random.key(seed), 7)
    tokens = normal_values(seeds[0], (TOKENS, D), 1.0, 6.0, ((0, 128),))
    expert_ids = draw_expert_ids(jax.random.fold_in(seeds[6], 71), 0)
    router_weights = jnp.clip(jnp.exp(math.log(1.0) - 1.6133518 * jax.random.uniform(seeds[2], (TOKENS, TOPK), jnp.float32) ** shard_levels(seeds[2], (TOKENS, TOPK), ((0, 128),), -0.2, 0.2)), 0.19921875, 1.0).astype(jnp.bfloat16)
    w_gate = normal_values(seeds[3], (EXPERTS, D, FF), D ** -0.5, 0.125, ((0, 128),))
    w_up = normal_values(seeds[4], (EXPERTS, D, FF), D ** -0.5, 0.125, ((0, 128),))
    w_down = normal_values(seeds[5], (EXPERTS, FF, D), FF ** -0.5, 0.21875, ((0, 128), (2, 8)))
    return {"tokens": tokens, "expert_ids": expert_ids, "router_weights": router_weights, "w_gate": w_gate, "w_up": w_up, "w_down": w_down}


def reference(tokens, expert_ids, router_weights, w_gate, w_up, w_down):
    block_count = TOKENS // TOK_DEV
    entry_total = TOKENS * TOPK
    expert_block = expert_ids.reshape(block_count, TOK_DEV * TOPK)
    hit_table = (expert_block[:, :, None] == jnp.arange(EXPERTS, dtype=jnp.int32)[None, None, :]).astype(jnp.int32)
    slot_rank = (jnp.sum(jnp.cumsum(hit_table, axis=1) * hit_table, axis=2) - 1).astype(jnp.int32)
    slot_index = (jnp.arange(block_count, dtype=jnp.int32)[:, None] * CAP + slot_rank).reshape(-1).astype(jnp.int32)
    token_row = (jnp.arange(entry_total, dtype=jnp.int32) // TOPK).astype(jnp.int32)
    flat_expert = expert_ids.reshape(-1).astype(jnp.int32)
    slot_width = block_count * CAP
    row_table = jnp.full((EXPERTS, slot_width), TOKENS, jnp.int32).at[flat_expert, slot_index].set(token_row)
    scale_table = jnp.zeros((EXPERTS, slot_width), jnp.float32).at[flat_expert, slot_index].set(
        router_weights.reshape(-1).astype(jnp.float32))
    padded = jnp.concatenate([tokens, jnp.zeros((1, D), tokens.dtype)], axis=0)

    def one_expert(running, expert_inputs):
        row_ids, gate_scale, gate_matrix, up_matrix, down_matrix = expert_inputs
        chosen = padded[row_ids]
        gate_act = jnp.dot(chosen, gate_matrix, preferred_element_type=jnp.float32)
        upward = jnp.dot(chosen, up_matrix, preferred_element_type=jnp.float32)
        hidden = (jax.nn.silu(gate_act) * upward).astype(jnp.bfloat16)
        expert_out = jnp.dot(hidden, down_matrix, preferred_element_type=jnp.float32)
        rounded = lax.optimization_barrier(expert_out.astype(jnp.bfloat16)).astype(jnp.float32)
        running = running.at[row_ids].add(gate_scale[:, None] * rounded)
        return running, None

    start_sum = jnp.zeros((TOKENS + 1, D), jnp.float32)
    running, _ = lax.scan(one_expert, start_sum, (row_table, scale_table, w_gate, w_up, w_down))
    return running[:TOKENS].astype(jnp.bfloat16)
```

```python
import jax
import jax.numpy as jnp
from jax import lax
from jax.experimental import pallas as pl
from jax.experimental.pallas import tpu as pltpu
from jax.sharding import PartitionSpec as P

MESH = pl.DeviceIdType.MESH
F32 = jnp.float32
BF16 = jnp.bfloat16
RING = 8
CAP = 24
ROWS = 2 * CAP
POS = {0: 0, 1: 1, 7: 2, 2: 3, 6: 4, 3: 5, 5: 6, 4: 7}
OFFSETS = (6, 2, 0, 7, 1)
IN_SLICES = (0, 4, 1, 5, 7, 3, 2, 6)
BACK = ((1, 1, 3), (5, 1, 6), (7, 7, 4), (3, 7, 7), (2, 2, 0), (6, 6, 1))
BACK_SELF = ((0, 2), (4, 5))


def kernel(meta, tok, wg, wu, wd, o_ref,
           xa, xb, sel, selw, xs, xr, wgs, wus, wds, hid, ob, yr, pk, pp, sp, sm, rp, rm, fs, fr, tri,
           lsem, wsem, zs, zr, cs, cr, ds_s, ds_r, xs_s, xs_r, bs, br, ps, pr, rps, rpr, rms, rmr, fsem):
    g = lax.axis_index("grp")
    l = lax.axis_index("loc")
    t = lax.axis_index("tp")
    z = g // 2
    c = g % 2
    other = 1 - c
    tok_rows = tok.shape[0]
    width = o_ref.shape[1]
    ff = wds.shape[1]
    half_ff = ff // 2

    def z_to(step):
        return {"grp": ((z + step) % RING) * 2 + c}

    def y_to(step):
        return {"loc": (l + step) % RING}

    def x_to(step):
        return {"tp": (t + step) % RING}

    partner = {"grp": z * 2 + other}

    def remote(src, dst, send, recv, dev):
        return pltpu.make_async_remote_copy(
            src_ref=src, dst_ref=dst, send_sem=send, recv_sem=recv, device_id=dev, device_id_type=MESH
        )

    started = []

    def go(copy):
        copy.start()
        started.append(copy)

    def cols(off):
        return pl.ds(pl.multiple_of(((l + off) % RING) * width, width), width)

    load_a = pltpu.make_async_copy(tok.at[:, cols(0)], xa.at[0, c, pl.ds(0, tok_rows), :], lsem.at[0])
    load_b = pltpu.make_async_copy(tok.at[:, cols(4)], xb.at[0, c], lsem.at[1])
    load_m = pltpu.make_async_copy(meta, xa.at[0, c, pl.ds(tok_rows, 16), :], lsem.at[2])
    load_d = pltpu.make_async_copy(wd.at[0], wds.at[0], lsem.at[3])
    for copy in (load_a, load_m, load_b, load_d):
        copy.start()
    weight_loads = []
    for i, off in enumerate(IN_SLICES):
        for j, (src, dst) in enumerate(((wg, wgs), (wu, wus))):
            copy = pltpu.make_async_copy(src.at[0, cols(off), :], dst.at[pl.ds(i * width, width), :], wsem.at[j, i])
            copy.start()
            weight_loads.append(copy)

    barrier = pltpu.get_barrier_semaphore()
    peers = [z_to(1), z_to(7), partner, y_to(1), y_to(7), y_to(2), y_to(6), y_to(4), x_to(1), x_to(7)]
    for peer in peers:
        pl.semaphore_signal(barrier, inc=1, device_id=peer, device_id_type=MESH)
    pl.semaphore_wait(barrier, len(peers))

    halves = (xa, xb)

    def z_copy(dz, h, step):
        to = (dz - step) % RING
        return remote(
            halves[h].at[POS[dz % RING], c], halves[h].at[POS[to], c],
            zs.at[h, POS[to]], zr.at[h, POS[to]], z_to(step),
        )

    def c_copy(dz, h):
        p = POS[dz % RING]
        return remote(halves[h].at[p, c], halves[h].at[p, c], cs.at[h, p], cr.at[h, p], partner)

    def d_copy(rel, h, step):
        to = (rel - step) % RING
        rows = pl.ds(h * half_ff, half_ff)
        return remote(
            wds.at[rel % RING, rows, :], wds.at[to, rows, :], ds_s.at[h, to], ds_r.at[h, to], x_to(step)
        )

    def z_event(step, h):
        dirs = []
        if step < 4 or h == 0:
            dirs.append((1, -step))
        if step < 4 or h == 1:
            dirs.append((-1, step))
        for way, dz in dirs:
            if step > 0:
                z_copy(dz + way, h, way).wait_recv()
            if step < 3 or (step == 3 and (h == 0) == (way == 1)):
                go(z_copy(dz, h, way))
            if step > 0 or way == 1:
                go(c_copy(dz, h))

    def x_event(step, h):
        dirs = []
        if step < 4 or h == 0:
            dirs.append((1, -step))
        if step < 4 or h == 1:
            dirs.append((-1, step))
        for way, rel in dirs:
            if step > 0:
                d_copy(rel + way, h, way).wait_recv()
            if step < 3 or (step == 3 and (h == 0) == (way == 1)):
                go(d_copy(rel, h, way))

    row_ids = lax.broadcasted_iota(jnp.int32, (8, 1), 0)
    offs = jnp.zeros((8, 1), jnp.int32)
    for j, off in enumerate(OFFSETS):
        offs = jnp.where(row_ids == j, off, offs)
    locs = l + offs
    locs = jnp.where(locs >= RING, locs - RING, locs)
    targets = jnp.where(row_ids < len(OFFSETS), g * RING + locs, -1).astype(F32)
    slot_ids = lax.broadcasted_iota(jnp.int32, (ROWS, tok_rows), 0).astype(F32)

    OUT = ((1, 4 * ROWS, 0, 4, 2), (7, 3 * ROWS, 2, 2, 2), (6, 0, 4, 6, 1), (2, ROWS, 5, 7, 1))

    def y_copy(p, k):
        off, _, src, dst, n = OUT[k]
        return remote(
            xs.at[p, :, pl.ds(src * width, n * width)], xr.at[p, :, pl.ds(dst * width, n * width)],
            xs_s.at[k, p], xs_r.at[k, p], y_to(off),
        )

    def select(dz):
        p = POS[dz]
        for h in range(2):
            c_copy(dz, h).wait_recv()
        hits = []
        weights = []
        for core in range(2):
            info = xa[p, core, pl.ds(tok_rows, 16), :].astype(F32)
            hit = jnp.zeros((8, tok_rows), F32)
            weight = jnp.zeros((8, tok_rows), F32)
            for k in range(8):
                same = info[k:k + 1, :] == targets
                hit = jnp.where(same, 1.0, hit)
                weight = jnp.where(same, info[8 + k:9 + k, :], weight)
            hits.append(hit)
            weights.append(weight)
        both = jnp.concatenate(hits, axis=0)
        rank = jnp.dot(both.astype(BF16), tri[...], preferred_element_type=F32)
        for core in range(2):
            place = jnp.where(hits[core] > 0.5, rank[8 * core:8 * core + 8, :] + float(core * CAP), -1.0)
            for j in range(len(OFFSETS)):
                same = slot_ids == place[j:j + 1, :]
                where = (p, pl.ds(j * ROWS, ROWS), pl.ds(core * tok_rows, tok_rows))
                sel[where] = jnp.where(same, 1.0, 0.0).astype(BF16)
                selw[where] = jnp.where(same, weights[core][j:j + 1, :], 0.0).astype(BF16)
        first = sel[p, :, pl.ds(0, tok_rows)]
        second = sel[p, :, pl.ds(tok_rows, tok_rows)]
        x0 = (
            jnp.dot(first, xa[p, 0, pl.ds(0, tok_rows), :], preferred_element_type=F32)
            + jnp.dot(second, xa[p, 1, pl.ds(0, tok_rows), :], preferred_element_type=F32)
        ).astype(BF16)
        x1 = (
            jnp.dot(first[2 * ROWS:, :], xb[p, 0], preferred_element_type=F32)
            + jnp.dot(second[2 * ROWS:, :], xb[p, 1], preferred_element_type=F32)
        ).astype(BF16)
        for k, (_, row, src, _, n) in enumerate(OUT):
            xs[p, :, pl.ds(src * width, width)] = x0[row:row + ROWS, :]
            if n == 2:
                xs[p, :, pl.ds((src + 1) * width, width)] = x1[row - 2 * ROWS:row - ROWS, :]
            go(y_copy(p, k))
        xr[p, :, pl.ds(0, width)] = x0[2 * ROWS:3 * ROWS, :]
        xr[p, :, pl.ds(width, width)] = x1[:ROWS, :]

    def gate_up(first, count):
        for p in range(first, first + count):
            for k in range(4):
                y_copy(p, k).wait_recv()
        x = xr[pl.ds(first, count)].reshape(count * ROWS, RING * width)
        rows = pl.ds(first * ROWS, count * ROWS)
        for n in range(ff // 256):
            part = pl.ds(n * 256, 256)
            gate = jnp.dot(x, wgs[:, part], preferred_element_type=F32)
            up = jnp.dot(x, wus[:, part], preferred_element_type=F32)
            hid[rows, part] = (gate / (1.0 + jnp.exp(-gate)) * up).astype(BF16)

    load_a.wait()
    load_m.wait()
    z_event(0, 0)
    load_b.wait()
    z_event(0, 1)
    load_d.wait()
    x_event(0, 0)
    x_event(0, 1)
    tri[...] = jnp.where(
        lax.broadcasted_iota(jnp.int32, (tok_rows, tok_rows), 0) < lax.broadcasted_iota(jnp.int32, (tok_rows, tok_rows), 1),
        1.0, 0.0,
    ).astype(BF16)
    select(0)
    z_event(1, 0)
    x_event(1, 0)
    z_event(1, 1)
    select(1)
    select(7)
    x_event(1, 1)
    z_event(2, 0)
    z_event(2, 1)
    x_event(2, 0)
    select(2)
    select(6)
    for copy in weight_loads:
        copy.wait()
    z_event(3, 0)
    gate_up(0, 3)
    x_event(2, 1)
    z_event(3, 1)
    select(3)
    select(5)
    z_event(4, 0)
    z_event(4, 1)
    x_event(3, 0)
    select(4)
    gate_up(3, 2)
    x_event(3, 1)
    gate_up(5, 3)
    x_event(4, 0)
    x_event(4, 1)

    def b_copy(p, k):
        _, off, window = BACK[k]
        return remote(ob.at[p, k], yr.at[p, window], bs.at[k, p], br.at[k, p], y_to(off))

    def down(first, count):
        h = hid[pl.ds(first * ROWS, count * ROWS), :]
        for k, (off, _, _) in enumerate(BACK):
            y = jnp.dot(h, wds[(l + off + RING - t) % RING], preferred_element_type=F32).astype(BF16)
            for i in range(count):
                ob[first + i, k] = y[i * ROWS:(i + 1) * ROWS, :]
        for p in reversed(range(first, first + count)):
            for k in range(len(BACK)):
                go(b_copy(p, k))
        for off, window in BACK_SELF:
            y = jnp.dot(h, wds[(l + off + RING - t) % RING], preferred_element_type=F32).astype(BF16)
            for i in range(count):
                yr[first + i, window] = y[i * ROWS:(i + 1) * ROWS, :]

    down(5, 3)
    down(3, 2)
    down(0, 3)

    def p_copy(dz):
        p = POS[dz]
        return remote(pk.at[p, other], pp.at[p], ps.at[p], pr.at[p], partner)

    def mix(dz):
        p = POS[dz]
        for k in range(len(BACK)):
            b_copy(p, k).wait_recv()
        for h, (row, lo, n) in enumerate(((0, 0, 5), (2 * ROWS, 5, 3))):
            part = lax.dot_general(
                selw[p, pl.ds(row, n * ROWS), :], yr[p, pl.ds(lo, n)].reshape(n * ROWS, width),
                (((0,), (0,)), ((), ())), preferred_element_type=F32,
            ).astype(BF16)
            pk[p, 0, h] = part[:tok_rows, :]
            pk[p, 1, h] = part[tok_rows:, :]
        go(p_copy(dz))

    def chip_sum(dz, h):
        p = POS[dz]
        return pk[p, c, h].astype(F32) + pp[p, h].astype(F32)

    def r_copy(way, s, h):
        src, dst, send, recv = (sp, rp, rps, rpr) if way == 1 else (sm, rm, rms, rmr)
        return remote(src.at[s - 1, h], dst.at[s - 1, h], send.at[s - 1, h], recv.at[s - 1, h], z_to(way))

    def ring(way, s, h):
        value = chip_sum(s if way == 1 else RING - s, h)
        if s < 3 or (s == 3 and (h == 0) == (way == 1)):
            r_copy(way, s + 1, h).wait_recv()
            value += (rp if way == 1 else rm)[s, h].astype(F32)
        (sp if way == 1 else sm)[s - 1, h] = value.astype(BF16)
        go(r_copy(way, s, h))

    mix(4)
    mix(3)
    p_copy(4).wait_recv()
    ring(1, 4, 0)
    ring(-1, 4, 1)
    mix(5)
    p_copy(3).wait_recv()
    p_copy(5).wait_recv()
    ring(1, 3, 1)
    ring(-1, 3, 0)
    mix(2)
    mix(6)
    ring(1, 3, 0)
    ring(-1, 3, 1)
    p_copy(2).wait_recv()
    p_copy(6).wait_recv()
    mix(1)
    mix(7)
    ring(1, 2, 1)
    ring(-1, 2, 1)
    ring(1, 2, 0)
    ring(-1, 2, 0)
    mix(0)
    p_copy(1).wait_recv()
    p_copy(7).wait_recv()
    ring(1, 1, 1)
    ring(-1, 1, 1)
    ring(1, 1, 0)
    ring(-1, 1, 0)
    p_copy(0).wait_recv()

    def total(h):
        value = chip_sum(0, h)
        for way, buf in ((1, rp), (-1, rm)):
            r_copy(way, 1, h).wait_recv()
            value += buf[0, h].astype(F32)
        return value

    last = remote(fs, fr, fsem.at[0], fsem.at[1], y_to(4))
    fs[...] = total(1).astype(BF16)
    go(last)
    own = total(0)
    last.wait_recv()
    o_ref[...] = (own + fr[...].astype(F32)).astype(BF16)
    for copy in started:
        copy.wait_send()


def body(tokens, expert_ids, router_weights, w_gate, w_up, w_down):
    rows, width_model = tokens.shape
    ff = w_gate.shape[2]
    width = width_model // RING
    meta = jnp.concatenate([expert_ids.T.astype(BF16), router_weights.T], axis=0)
    dma = pltpu.SemaphoreType.DMA
    anywhere = pl.BlockSpec(memory_space=pl.ANY)
    return pl.pallas_call(
        kernel,
        out_shape=jax.ShapeDtypeStruct((rows, width), BF16),
        in_specs=[anywhere] * 5,
        out_specs=pl.BlockSpec(memory_space=pltpu.VMEM),
        scratch_shapes=[
            pltpu.VMEM((8, 2, rows + 16, width), BF16),
            pltpu.VMEM((8, 2, rows, width), BF16),
            pltpu.VMEM((8, 5 * ROWS, 2 * rows), BF16),
            pltpu.VMEM((8, 5 * ROWS, 2 * rows), BF16),
            pltpu.VMEM((8, ROWS, 6 * width), BF16),
            pltpu.VMEM((8, ROWS, 8 * width), BF16),
            pltpu.VMEM((width_model, ff), BF16),
            pltpu.VMEM((width_model, ff), BF16),
            pltpu.VMEM((8, ff, width), BF16),
            pltpu.VMEM((8 * ROWS, ff), BF16),
            pltpu.VMEM((8, 6, ROWS, width), BF16),
            pltpu.VMEM((8, 8, ROWS, width), BF16),
            pltpu.VMEM((8, 2, 2, rows, width), BF16),
            pltpu.VMEM((8, 2, rows, width), BF16),
            pltpu.VMEM((4, 2, rows, width), BF16),
            pltpu.VMEM((4, 2, rows, width), BF16),
            pltpu.VMEM((4, 2, rows, width), BF16),
            pltpu.VMEM((4, 2, rows, width), BF16),
            pltpu.VMEM((rows, width), BF16),
            pltpu.VMEM((rows, width), BF16),
            pltpu.VMEM((rows, rows), BF16),
            dma((4,)), dma((2, 8)),
            dma((2, 8)), dma((2, 8)), dma((2, 8)), dma((2, 8)),
            dma((2, 8)), dma((2, 8)), dma((4, 8)), dma((4, 8)),
            dma((6, 8)), dma((6, 8)), dma((8,)), dma((8,)),
            dma((4, 2)), dma((4, 2)), dma((4, 2)), dma((4, 2)), dma((2,)),
        ],
        compiler_params=pltpu.CompilerParams(
            collective_id=0, has_side_effects=True, vmem_limit_bytes=60 * 1024 * 1024
        ),
    )(meta, tokens, w_gate, w_up, w_down)


def solution(mesh):
    placed = (
        P(("grp", "tp"), None),
        P(("grp", "tp"), None),
        P(("grp", "tp"), None),
        P(("grp", "loc"), None, None),
        P(("grp", "loc"), None, None),
        P(("grp", "loc"), None, "tp"),
    )
    return jax.shard_map(
        body, mesh=mesh, in_specs=placed, out_specs=P(("grp", "tp"), "loc"), check_vma=False
    )
```

```python
import jax
import jax.numpy as jnp
from jax import lax
from jax.experimental import pallas as pl
from jax.experimental.pallas import tpu as pltpu
from jax.sharding import PartitionSpec as P

MESH = pl.DeviceIdType.MESH
F32 = jnp.float32
BF16 = jnp.bfloat16
RING = 8
CAP = 24
ROWS = 2 * CAP
Z_PARTS = 2
X_PARTS = 2
R_PARTS = 2
POS = {0: 0, 1: 1, 7: 2, 2: 3, 6: 4, 3: 5, 5: 6, 4: 7}
OFFSETS = (6, 2, 0, 7, 1)
IN_SLICES = (0, 4, 1, 5, 7, 3, 2, 6)
BACK = ((1, 1, 3), (5, 1, 6), (7, 7, 4), (3, 7, 7), (2, 2, 0), (6, 6, 1))
BACK_SELF = ((0, 2), (4, 5))


def kernel(ids, gains, tok, wg, wu, wd, o_ref,
           xa, xb, sel, selw, xs, xr, wgs, wus, wds, hid, ob, yr, pk, pp, sp, sm, rp, rm, fs, fr, fa, tri, ids_v, gains_v,
           lsem, wsem, zs, zr, cs, cr, ds_s, ds_r, xs_s, xs_r, bs, br, ps, pr, rps, rpr, rms, rmr, fsem):
    g = lax.axis_index("grp")
    l = lax.axis_index("loc")
    t = lax.axis_index("tp")
    z = g // 2
    c = g % 2
    other = 1 - c
    tok_rows = tok.shape[0]
    width = o_ref.shape[1]
    ff = wds.shape[1]
    piece_ff = ff // (2 * X_PARTS)
    piece = tok_rows // R_PARTS

    def z_to(step):
        return {"grp": ((z + step) % RING) * 2 + c}

    def y_to(step):
        return {"loc": (l + step) % RING}

    def x_to(step):
        return {"tp": (t + step) % RING}

    partner = {"grp": z * 2 + other}

    def remote(src, dst, send, recv, dev):
        return pltpu.make_async_remote_copy(
            src_ref=src, dst_ref=dst, send_sem=send, recv_sem=recv, device_id=dev, device_id_type=MESH
        )

    started = []

    def go(copy):
        copy.start()
        started.append(copy)

    def cols(off):
        return pl.ds(pl.multiple_of(((l + off) % RING) * width, width), width)

    load_a = pltpu.make_async_copy(tok.at[:, cols(0)], xa.at[0, c, pl.ds(0, tok_rows), :], lsem.at[0])
    load_b = pltpu.make_async_copy(tok.at[:, cols(4)], xb.at[0, c], lsem.at[1])
    load_i = pltpu.make_async_copy(ids, ids_v, lsem.at[2])
    load_g = pltpu.make_async_copy(gains, gains_v, lsem.at[4])
    load_d = pltpu.make_async_copy(wd.at[0], wds.at[0], lsem.at[3])
    for copy in (load_d, load_b, load_i, load_g, load_a):
        copy.start()
    weight_loads = []
    for i, off in enumerate(IN_SLICES):
        for j, (src, dst) in enumerate(((wg, wgs), (wu, wus))):
            copy = pltpu.make_async_copy(src.at[0, cols(off), :], dst.at[pl.ds(i * width, width), :], wsem.at[j, i])
            weight_loads.append(copy)

    barrier = pltpu.get_barrier_semaphore()
    peers = [z_to(1), z_to(7), partner, y_to(1), y_to(7), y_to(2), y_to(6), x_to(1), x_to(7)]
    for peer in peers:
        pl.semaphore_signal(barrier, inc=1, device_id=peer, device_id_type=MESH)
    pl.semaphore_wait(barrier, len(peers))

    halves = (xa, xb)

    def z_copy(dz, h, r, step):
        to = (dz - step) % RING
        size = tok_rows // Z_PARTS
        extra = 16 if h == 0 and r == Z_PARTS - 1 else 0
        rows = pl.ds(r * size, size + extra)
        return remote(
            halves[h].at[POS[dz % RING], c, rows, :], halves[h].at[POS[to], c, rows, :],
            zs.at[h, r, POS[to]], zr.at[h, r, POS[to]], z_to(step),
        )

    def c_copy(dz, h):
        p = POS[dz % RING]
        return remote(halves[h].at[p, c], halves[h].at[p, c], cs.at[h, p], cr.at[h, p], partner)

    def d_copy(rel, q, step):
        to = (rel - step) % RING
        rows = pl.ds(q * piece_ff, piece_ff)
        return remote(
            wds.at[rel % RING, rows, :], wds.at[to, rows, :], ds_s.at[q, to], ds_r.at[q, to], x_to(step)
        )

    def ways(step, h):
        found = []
        if step < 4 or h == 0:
            found.append((1, -step))
        if step < 4 or h == 1:
            found.append((-1, step))
        return found

    def goes_on(step, h, way):
        return step < 3 or (step == 3 and (h == 0) == (way == 1))

    def z_event(step, h):
        for r in range(Z_PARTS):
            for way, dz in ways(step, h):
                if step > 0:
                    z_copy(dz + way, h, r, way).wait_recv()
                if goes_on(step, h, way):
                    go(z_copy(dz, h, r, way))
        for way, dz in ways(step, h):
            if step > 0 or way == 1:
                go(c_copy(dz, h))

    def x_event(step, h):
        for q in range(h * X_PARTS, (h + 1) * X_PARTS):
            for way, rel in ways(step, h):
                if step > 0:
                    d_copy(rel + way, q, way).wait_recv()
                if goes_on(step, h, way):
                    go(d_copy(rel, q, way))

    row_ids = lax.broadcasted_iota(jnp.int32, (8, 1), 0)
    offs = jnp.zeros((8, 1), jnp.int32)
    for j, off in enumerate(OFFSETS):
        offs = jnp.where(row_ids == j, off, offs)
    locs = l + offs
    locs = jnp.where(locs >= RING, locs - RING, locs)
    targets = jnp.where(row_ids < len(OFFSETS), g * RING + locs, -1).astype(F32)
    slot_ids = lax.broadcasted_iota(jnp.int32, (ROWS, tok_rows), 0).astype(F32)

    OUT = ((1, 4 * ROWS, 0, 4, 2), (7, 3 * ROWS, 2, 2, 2), (6, 0, 4, 6, 1), (2, ROWS, 5, 7, 1))

    def y_copy(p, k):
        off, _, src, dst, n = OUT[k]
        return remote(
            xs.at[p, :, pl.ds(src * width, n * width)], xr.at[p, :, pl.ds(dst * width, n * width)],
            xs_s.at[k, p], xs_r.at[k, p], y_to(off),
        )

    def select(dz):
        p = POS[dz]
        for h in range(2):
            c_copy(dz, h).wait_recv()
        hits = []
        weights = []
        for core in range(2):
            info = xa[p, core, pl.ds(tok_rows, 16), :].astype(F32)
            hit = jnp.zeros((8, tok_rows), F32)
            weight = jnp.zeros((8, tok_rows), F32)
            for k in range(8):
                same = info[k:k + 1, :] == targets
                hit = jnp.where(same, 1.0, hit)
                weight = jnp.where(same, info[8 + k:9 + k, :], weight)
            hits.append(hit)
            weights.append(weight)
        both = jnp.concatenate(hits, axis=0)
        rank = jnp.dot(both.astype(BF16), tri[...], preferred_element_type=F32)
        for core in range(2):
            place = jnp.where(hits[core] > 0.5, rank[8 * core:8 * core + 8, :] + float(core * CAP), -1.0)
            for j in range(len(OFFSETS)):
                same = slot_ids == place[j:j + 1, :]
                where = (p, pl.ds(j * ROWS, ROWS), pl.ds(core * tok_rows, tok_rows))
                sel[where] = jnp.where(same, 1.0, 0.0).astype(BF16)
                selw[where] = jnp.where(same, weights[core][j:j + 1, :], 0.0).astype(BF16)
        first = sel[p, :, pl.ds(0, tok_rows)]
        second = sel[p, :, pl.ds(tok_rows, tok_rows)]
        x0 = (
            jnp.dot(first, xa[p, 0, pl.ds(0, tok_rows), :], preferred_element_type=F32)
            + jnp.dot(second, xa[p, 1, pl.ds(0, tok_rows), :], preferred_element_type=F32)
        ).astype(BF16)
        x1 = (
            jnp.dot(first[2 * ROWS:, :], xb[p, 0], preferred_element_type=F32)
            + jnp.dot(second[2 * ROWS:, :], xb[p, 1], preferred_element_type=F32)
        ).astype(BF16)
        for k, (_, row, src, _, n) in enumerate(OUT):
            xs[p, :, pl.ds(src * width, width)] = x0[row:row + ROWS, :]
            if n == 2:
                xs[p, :, pl.ds((src + 1) * width, width)] = x1[row - 2 * ROWS:row - ROWS, :]
            go(y_copy(p, k))
        xr[p, :, pl.ds(0, width)] = x0[2 * ROWS:3 * ROWS, :]
        xr[p, :, pl.ds(width, width)] = x1[:ROWS, :]

    def gate_up(first, count):
        for p in range(first, first + count):
            for k in range(4):
                y_copy(p, k).wait_recv()
        x = xr[pl.ds(first, count)].reshape(count * ROWS, RING * width)
        rows = pl.ds(first * ROWS, count * ROWS)
        for n in range(ff // 256):
            part = pl.ds(n * 256, 256)
            gate = jnp.dot(x, wgs[:, part], preferred_element_type=F32)
            up = jnp.dot(x, wus[:, part], preferred_element_type=F32)
            hid[rows, part] = (gate / (1.0 + jnp.exp(-gate)) * up).astype(BF16)

    load_d.wait()
    x_event(0, 0)
    x_event(0, 1)
    load_b.wait()
    z_event(0, 1)
    load_i.wait()
    load_g.wait()
    xa[0, c, pl.ds(tok_rows, 16), :] = jnp.concatenate(
        [ids_v[...].astype(F32), gains_v[...].astype(F32)], axis=0
    ).astype(BF16)
    tri[...] = jnp.where(
        lax.broadcasted_iota(jnp.int32, (tok_rows, tok_rows), 0) < lax.broadcasted_iota(jnp.int32, (tok_rows, tok_rows), 1),
        1.0, 0.0,
    ).astype(BF16)
    load_a.wait()
    z_event(0, 0)
    for copy in weight_loads:
        copy.start()
    select(0)
    z_event(1, 1)
    x_event(1, 0)
    z_event(1, 0)
    select(1)
    select(7)
    x_event(1, 1)
    z_event(2, 1)
    z_event(2, 0)
    x_event(2, 0)
    select(2)
    select(6)
    z_event(3, 1)
    for copy in weight_loads:
        copy.wait()
    x_event(2, 1)
    z_event(3, 0)
    gate_up(0, 3)
    select(3)
    select(5)
    z_event(4, 1)
    z_event(4, 0)
    x_event(3, 0)
    select(4)
    gate_up(3, 2)
    x_event(3, 1)
    gate_up(5, 2)

    def b_copy(p, k):
        rel, off, window = BACK[k]
        return remote(ob.at[p, rel], yr.at[p, window], bs.at[k, p], br.at[k, p], y_to(off))

    def down(slot, first, count):
        h = hid[pl.ds(first * ROWS, count * ROWS), :]
        y = jnp.dot(h, wds[slot], preferred_element_type=F32).astype(BF16)
        rel = (t + slot + RING - l) % RING
        for i in range(count):
            ob[first + i, rel] = y[i * ROWS:(i + 1) * ROWS, :]

    def send_back(first, count):
        for p in reversed(range(first, first + count)):
            for k in range(len(BACK)):
                go(b_copy(p, k))

    early = (0, 1, 7, 2, 6, 3, 5)
    for slot in early:
        down(slot, 0, 7)
    gate_up(7, 1)
    for slot in early:
        down(slot, 7, 1)
    x_event(4, 0)
    x_event(4, 1)
    down(4, 5, 3)
    send_back(5, 3)
    down(4, 0, 5)
    send_back(0, 5)

    def p_copy(dz, h):
        p = POS[dz]
        return remote(pk.at[p, other, h], pp.at[p, h], ps.at[p, h], pr.at[p, h], partner)

    def mix(dz):
        p = POS[dz]
        for rel, window in BACK_SELF:
            yr[p, window] = ob[p, rel]
        for k in range(len(BACK)):
            b_copy(p, k).wait_recv()
        for h, row, lo, n in ((1, 2 * ROWS, 5, 3), (0, 0, 0, 5)):
            part = lax.dot_general(
                selw[p, pl.ds(row, n * ROWS), :], yr[p, pl.ds(lo, n)].reshape(n * ROWS, width),
                (((0,), (0,)), ((), ())), preferred_element_type=F32,
            ).astype(BF16)
            pk[p, 0, h] = part[:tok_rows, :]
            pk[p, 1, h] = part[tok_rows:, :]
            go(p_copy(dz, h))

    def rows_of(r):
        return pl.ds(r * piece, piece)

    def chip_sum(dz, h, r):
        p = POS[dz]
        return pk[p, c, h, rows_of(r), :].astype(F32) + pp[p, h, rows_of(r), :].astype(F32)

    def r_copy(way, s, h, r):
        src, dst, send, recv = (sp, rp, rps, rpr) if way == 1 else (sm, rm, rms, rmr)
        return remote(
            src.at[s - 1, h, rows_of(r), :], dst.at[s - 1, h, rows_of(r), :],
            send.at[s - 1, h, r], recv.at[s - 1, h, r], z_to(way),
        )

    def ring(s, h):
        sides = [way for way in (1, -1) if s < 4 or (h == 0) == (way == 1)]
        for way in sides:
            p_copy(s if way == 1 else RING - s, h).wait_recv()
        for r in range(R_PARTS):
            for way in sides:
                value = chip_sum(s if way == 1 else RING - s, h, r)
                if goes_on(s, h, way):
                    r_copy(way, s + 1, h, r).wait_recv()
                    value += (rp if way == 1 else rm)[s, h, rows_of(r), :].astype(F32)
                (sp if way == 1 else sm)[s - 1, h, rows_of(r), :] = value.astype(BF16)
                go(r_copy(way, s, h, r))

    def total(h, r):
        value = chip_sum(0, h, r)
        for way, buf in ((1, rp), (-1, rm)):
            r_copy(way, 1, h, r).wait_recv()
            value += buf[0, h, rows_of(r), :].astype(F32)
        return value

    def way_of(r):
        return y_to(2 if r < R_PARTS // 2 else 6)

    def f_copy(stage, r):
        src, dst = (fs, fa) if stage == 0 else (fa, fr)
        return remote(src.at[rows_of(r), :], dst.at[rows_of(r), :], fsem.at[0, stage, r], fsem.at[1, stage, r], way_of(r))

    mix(4)
    ring(4, 1)
    ring(4, 0)
    mix(3)
    mix(5)
    ring(3, 1)
    ring(3, 0)
    mix(2)
    mix(6)
    ring(2, 1)
    ring(2, 0)
    mix(1)
    mix(7)
    ring(1, 1)
    ring(1, 0)
    mix(0)
    p_copy(0, 1).wait_recv()
    p_copy(0, 0).wait_recv()
    for r in range(R_PARTS):
        fs[rows_of(r), :] = total(1, r).astype(BF16)
        go(f_copy(0, r))
    for r in range(R_PARTS):
        f_copy(0, r).wait_recv()
        go(f_copy(1, r))
    for r in range(R_PARTS):
        own = total(0, r)
        f_copy(1, r).wait_recv()
        o_ref[rows_of(r), :] = (own + fr[rows_of(r), :].astype(F32)).astype(BF16)
    for copy in started:
        copy.wait_send()


def body(tokens, expert_ids, router_weights, w_gate, w_up, w_down):
    rows, width_model = tokens.shape
    ff = w_gate.shape[2]
    width = width_model // RING
    dma = pltpu.SemaphoreType.DMA
    anywhere = pl.BlockSpec(memory_space=pl.ANY)
    return pl.pallas_call(
        kernel,
        out_shape=jax.ShapeDtypeStruct((rows, width), BF16),
        in_specs=[anywhere] * 6,
        out_specs=pl.BlockSpec(memory_space=pltpu.VMEM),
        scratch_shapes=[
            pltpu.VMEM((8, 2, rows + 16, width), BF16),
            pltpu.VMEM((8, 2, rows, width), BF16),
            pltpu.VMEM((8, 5 * ROWS, 2 * rows), BF16),
            pltpu.VMEM((8, 5 * ROWS, 2 * rows), BF16),
            pltpu.VMEM((8, ROWS, 6 * width), BF16),
            pltpu.VMEM((8, ROWS, 8 * width), BF16),
            pltpu.VMEM((width_model, ff), BF16),
            pltpu.VMEM((width_model, ff), BF16),
            pltpu.VMEM((8, ff, width), BF16),
            pltpu.VMEM((8 * ROWS, ff), BF16),
            pltpu.VMEM((8, 8, ROWS, width), BF16),
            pltpu.VMEM((8, 8, ROWS, width), BF16),
            pltpu.VMEM((8, 2, 2, rows, width), BF16),
            pltpu.VMEM((8, 2, rows, width), BF16),
            pltpu.VMEM((4, 2, rows, width), BF16),
            pltpu.VMEM((4, 2, rows, width), BF16),
            pltpu.VMEM((4, 2, rows, width), BF16),
            pltpu.VMEM((4, 2, rows, width), BF16),
            pltpu.VMEM((rows, width), BF16),
            pltpu.VMEM((rows, width), BF16),
            pltpu.VMEM((rows, width), BF16),
            pltpu.VMEM((rows, rows), BF16),
            pltpu.VMEM((8, rows), jnp.int32),
            pltpu.VMEM((8, rows), BF16),
            dma((5,)), dma((2, 8)),
            dma((2, Z_PARTS, 8)), dma((2, Z_PARTS, 8)), dma((2, 8)), dma((2, 8)),
            dma((2 * X_PARTS, 8)), dma((2 * X_PARTS, 8)), dma((4, 8)), dma((4, 8)),
            dma((6, 8)), dma((6, 8)), dma((8, 2)), dma((8, 2)),
            dma((4, 2, R_PARTS)), dma((4, 2, R_PARTS)), dma((4, 2, R_PARTS)), dma((4, 2, R_PARTS)),
            dma((2, 2, R_PARTS)),
        ],
        compiler_params=pltpu.CompilerParams(
            collective_id=0, has_side_effects=True, vmem_limit_bytes=60 * 1024 * 1024
        ),
    )(expert_ids.T, router_weights.T, tokens, w_gate, w_up, w_down)


def solution(mesh):
    placed = (
        P(("grp", "tp"), None),
        P(("grp", "tp"), None),
        P(("grp", "tp"), None),
        P(("grp", "loc"), None, None),
        P(("grp", "loc"), None, None),
        P(("grp", "loc"), None, "tp"),
    )
    return jax.shard_map(
        body, mesh=mesh, in_specs=placed, out_specs=P(("grp", "tp"), "loc"), check_vma=False
    )
```
